32 devices in a mesh: freq: 4 (over z), pts: 8 (over y, x, core).
Axes of the slice: x: 2, y: 2, z: 4, core: 2. Of those that a mesh axis runs over, the one named last changes fastest.
Arguments:
- histories: float32 [8, 2048, 4096], P(None, ('freq', 'pts')), may hold values from -6 to 6
- point_weight: float32 [4096], P('pts'), may hold values from 0.5 to 2
- basis: float32 [4096, 4096], P('pts', 'freq'), may hold values from -0.09375 to 0.09375
Outputs:
- coeffs: float32 [8, 2, 256, 4096], P(None, None, 'freq', 'pts')
The draws below stay inside these ranges and needn't reach their ends.
All inputs are finite; a program needn't handle non-finite values.
Results may differ from the reference program's by a relative error of at most 0.00011.
Values sent between devices are 32-bit elements; how exact they have to be, the bound alone decides.
A program may use at most 128 MiB of HBM per device.

```python
import math
import jax
import jax.numpy as jnp
from jax import lax

NT = 2048
F = 256
H = 4096
CASES = 8
P_SIZE = 4096


def level_of(own_key, shape, cuts, least, largest):
    def one(dim, shards_of):
        heights = jax.random.uniform(jax.random.fold_in(jax.random.fold_in(own_key, 6), dim), (shards_of,), jnp.float32, least / len(cuts), largest / len(cuts))
        return jnp.repeat(jnp.exp(heights), shape[dim] // shards_of).reshape((-1,) + (1,) * (len(shape) - dim - 1))

    factor_of = one(*cuts[0])
    for cut in cuts[1:]:
        factor_of = factor_of * one(*cut)
    return factor_of


def noise(key, extent, scale, limit, split=(), kind=jnp.bfloat16):
    values = scale * jax.random.normal(key, extent, jnp.float32)
    if split:
        values = values * level_of(key, extent, split, -0.22, 0.18)
    return jnp.clip(values, -limit, limit).astype(kind)


def setup_inputs(seed: int = 0) -> dict:
    splits = jax.random.split(jax.random.key(seed), 4)
    histories = noise(splits[0], (CASES, NT, P_SIZE), 1.0, 6.0, ((1, 32),), jnp.float32)
    point_weight = jnp.clip(jnp.exp(math.log(2.0) - 1.3862944 * jax.random.uniform(splits[1], (P_SIZE,), jnp.float32) ** level_of(splits[1], (P_SIZE,), ((0, 8),), -0.2, 0.2)), 0.5, 2.0)
    basis = noise(splits[2], (P_SIZE, H), P_SIZE ** -0.5, 0.09375, ((0, 8), (1, 4)), jnp.float32)
    return dict(histories=histories, point_weight=point_weight, basis=basis)


def make_table(times, total, bins):
    freqs = jnp.arange(1, bins + 1, dtype=jnp.int32)
    phase_int = times[:, None] * freqs[None, :] % total
    angle = 2.0 * jnp.pi / total * phase_int.astype(jnp.float32)
    window = 0.5 - 0.5 * jnp.cos(2.0 * jnp.pi / total * times.astype(jnp.float32))
    scale = (window / jnp.sqrt(jnp.float32(total)))[:, None]
    return jnp.concatenate([jnp.cos(angle) * scale, -jnp.sin(angle) * scale], axis=1)

def reference(histories, point_weight, basis):
    table = make_table(jnp.arange(NT, dtype=jnp.int32), NT, F)
    spectrum = jnp.einsum('stp,tk->skp', histories, table, precision=lax.Precision.HIGHEST)
    weighted = (spectrum * point_weight[None, None, :]).reshape(CASES * 2 * F, P_SIZE)
    coeffs = jnp.dot(weighted, basis, precision=lax.Precision.HIGHEST, preferred_element_type=jnp.float32)
    return coeffs.reshape(CASES, 2, F, H)
```

```python
import functools

import jax
import jax.numpy as jnp
from jax import lax
from jax.experimental import pallas as pl
from jax.experimental.pallas import tpu as pltpu
from jax.sharding import PartitionSpec as P

F = 256
LEAD = 2
AHEAD = 8
COLS = 128
RING = 2
MESH = pl.DeviceIdType.MESH


def make_table(times, total, bins, blocks):
    freqs = jnp.arange(1, bins + 1, dtype=jnp.int32)
    phase_int = freqs[:, None] * times[None, :] % total
    angle = 2.0 * jnp.pi / total * phase_int.astype(jnp.float32)
    window = 0.5 - 0.5 * jnp.cos(2.0 * jnp.pi / total * times.astype(jnp.float32))
    scale = (window / jnp.sqrt(jnp.float32(total)))[None, :]
    cos = (jnp.cos(angle) * scale).reshape(blocks, 1, bins // blocks, -1)
    sin = (-jnp.sin(angle) * scale).reshape(blocks, 1, bins // blocks, -1)
    return jnp.concatenate([cos, sin], axis=1).reshape(2 * bins, -1)


def split(x):
    high = x.astype(jnp.bfloat16)
    return high, (x - high.astype(jnp.float32)).astype(jnp.bfloat16)


def dot3(a, b):
    ah, al = a
    bh, bl = b
    dot = functools.partial(jnp.dot, preferred_element_type=jnp.float32)
    return dot(ah, bh) + (dot(ah, bl) + dot(al, bh))


def kernel(
    nf, np_, hist, table, weight, basis, out,
    h2, bas, rs, spec, wf, th, tl_, wh, wl, cown, csend, pland, fland,
    h_send, h_recv, h_own, b_send_r, b_send_l, b_recv, b_own,
    r_send, r_recv, p_send, p_recv, f_send, f_recv, o_sem,
):
    cases, time_local, _ = hist.shape
    points = h2.shape[2]
    rows = wh.shape[1]
    per = np_ // nf
    pieces = bas.shape[1]
    ho = pieces * COLS
    chunks = per * pieces
    chips = np_ // 2
    me = lax.axis_index("freq")
    p = lax.axis_index("pts")
    core = lax.rem(p, 2)
    chip = lax.div(p, 2)
    right, left = jnp.minimum(me + 1, nf - 1), jnp.maximum(me - 1, 0)
    has_r, has_l = me < nf - 1, me > 0

    barrier = pltpu.get_barrier_semaphore()
    for d in range(1, np_):
        pl.semaphore_signal(barrier, inc=1, device_id={"pts": lax.rem(p + d, np_)}, device_id_type=MESH)

    @pl.when(has_r)
    def _():
        pl.semaphore_signal(barrier, inc=1, device_id={"freq": right}, device_id_type=MESH)

    @pl.when(has_l)
    def _():
        pl.semaphore_signal(barrier, inc=1, device_id={"freq": left}, device_id_type=MESH)

    inner = jnp.logical_and(has_l, has_r)

    @pl.when(inner)
    def _():
        pl.semaphore_wait(barrier, np_ + 1)

    @pl.when(jnp.logical_not(inner))
    def _():
        pl.semaphore_wait(barrier, np_)

    def h_copy(s, q, slot):
        return pltpu.make_async_remote_copy(
            src_ref=hist.at[s, :, pl.ds(pl.multiple_of(q * points, 128), points)],
            dst_ref=h2.at[s, pl.ds(pl.multiple_of(slot * time_local, 8), time_local), :],
            send_sem=h_send.at[s, q], recv_sem=h_recv.at[s, slot],
            device_id={"pts": q}, device_id_type=MESH,
        )

    def h_local(s):
        return pltpu.make_async_copy(
            hist.at[s, :, pl.ds(pl.multiple_of(p * points, 128), points)],
            h2.at[s, pl.ds(pl.multiple_of(p * time_local, 8), time_local), :],
            h_own.at[s],
        )

    def h_start(s):
        for d in range(1, np_):
            h_copy(s, lax.rem(p + d, np_), p).start()
        h_local(s).start()

    def b_source(n):
        at = lax.rem(n, per) * ho + lax.div(n, per) * COLS
        return basis.at[:, pl.ds(pl.multiple_of(at, 128), COLS)]

    def b_place(b, n):
        return bas.at[b * per + lax.rem(n, per), lax.div(n, per)]

    def b_copy(b, n, to, sems, src=None):
        dst = b_place(b, n)
        return pltpu.make_async_remote_copy(
            src_ref=dst if src is None else src, dst_ref=dst,
            send_sem=sems.at[b, n], recv_sem=b_recv.at[b, n],
            device_id={"freq": to}, device_id_type=MESH,
        )

    def b_local(n):
        return pltpu.make_async_copy(b_source(n), b_place(me, n), b_own.at[n])

    def r_copy(s, g, dst, to):
        return pltpu.make_async_remote_copy(
            src_ref=rs.at[s, g], dst_ref=rs.at[s, dst], send_sem=r_send.at[s, g], recv_sem=r_recv.at[s, dst],
            device_id={"freq": to}, device_id_type=MESH,
        )

    def own(s, g):
        return spec[lax.rem(s, RING), pl.ds(pl.multiple_of(g * rows, 8), rows), :]

    def place_in(t, hops):
        u = t - 2 * hops + nf * (LEAD + 2)
        return lax.div(u, nf) - (LEAD + 2), lax.rem(u, nf)

    def forward(k, g, behind, ahead, has_ahead, to, sems, last):
        n = k + LEAD
        sums = jnp.logical_and(jnp.logical_and(has_ahead, ahead), jnp.logical_and(k >= 0, k < cases))

        @pl.when(sums)
        def _():
            @pl.when(behind)
            def _():
                r_copy(k, g, g, to).wait_recv()
                rs[k, g] = rs[k, g] + own(k, g)

            @pl.when(jnp.logical_not(behind))
            def _():
                rs[k, g] = own(k, g)

            if last is None:
                r_copy(k, g, g, to).start()
            else:
                @pl.when(last)
                def _():
                    r_copy(k, g, nf, to).start()

                @pl.when(jnp.logical_not(last))
                def _():
                    r_copy(k, g, g, to).start()

        chunk = jnp.logical_and(jnp.logical_not(ahead), jnp.logical_and(n >= 0, n < chunks))

        @pl.when(jnp.logical_and(chunk, g == me))
        def _():
            @pl.when(has_ahead)
            def _():
                b_copy(me, n, to, sems, b_source(n)).start()

        @pl.when(jnp.logical_and(chunk, g != me))
        def _():
            copy = b_copy(g, n, to, sems)
            copy.wait_recv()

            @pl.when(has_ahead)
            def _():
                copy.start()

    def send(t):
        k, r = place_in(t, me)
        g = nf - 1 - r
        forward(k, g, has_l, g > me, has_r, right, b_send_r, None)
        k, g = place_in(t, nf - 1 - me)
        forward(k, g, has_r, g < me, has_l, left, b_send_l, g == me - 1)

    def finalize(s):
        wf[...] = own(s, me)

        @pl.when(has_l)
        def _():
            r_copy(s, me, me, right).wait_recv()
            wf[...] = wf[...] + rs[s, me]

        @pl.when(has_r)
        def _():
            r_copy(s, nf, nf, left).wait_recv()
            wf[...] = wf[...] + rs[s, nf]

        high, low = split(wf[...] * weight[...])
        wh[s] = high
        wl[s] = low

    def p_copy(e, slot):
        return pltpu.make_async_remote_copy(
            src_ref=csend.at[slot], dst_ref=pland.at[e],
            send_sem=p_send.at[slot], recv_sem=p_recv.at[e],
            device_id={"pts": chip * 2 + 1 - core}, device_id_type=MESH,
        )

    def f_copy(e, c, slot):
        return pltpu.make_async_remote_copy(
            src_ref=pland.at[e, c], dst_ref=fland.at[e, slot], send_sem=f_send.at[e, c], recv_sem=f_recv.at[e, slot],
            device_id={"pts": c * 2 + core}, device_id_type=MESH,
        )

    def o_copy(e):
        s, m = lax.div(e, pieces), lax.rem(e, pieces)
        return pltpu.make_async_copy(
            pland.at[e, chip],
            out.at[pl.ds(pl.multiple_of(s * rows, 8), rows), pl.ds(pl.multiple_of(m * COLS, 128), COLS)],
            o_sem.at[e],
        )

    def compute(s, m, slot):
        lhs = wh[s], wl[s]
        for d in range(1, chips + 1):
            c = lax.rem(chip + d, chips)
            pair = jnp.concatenate([bas[c * 2 + 1 - core, m], bas[c * 2 + core, m]], axis=1)
            both = dot3(lhs, split(pair))
            csend[slot, c] = both[:, :COLS]
            cown[slot, c] = both[:, COLS:]
        p_copy(s * pieces + m, slot).start()

    def pass_on(s, m, slot):
        e = s * pieces + m
        copy = p_copy(e, slot)
        copy.wait_recv()
        copy.wait_send()
        pland[e] = pland[e] + cown[slot]
        for d in range(1, chips):
            f_copy(e, lax.rem(chip + d, chips), chip).start()

    across = -(-pieces // nf)

    def ready(i):
        return jnp.minimum(lax.div(i + LEAD - 1, per), pieces)

    def units(t, act):
        v = t - (nf - 2) + nf * (LEAD + 2)
        i, part = lax.div(v, nf) - (LEAD + 2), lax.rem(v, nf)
        s = i - 1

        @pl.when(jnp.logical_and(s >= 0, s < cases))
        def _():
            done = ready(i)
            low = lax.div(part * pieces, nf)
            high = jnp.minimum(lax.div((part + 1) * pieces, nf), done)

            def new_case(m, carry):
                act(s, m, m - low)
                return carry

            lax.fori_loop(low, high, new_case, 0)
            m_new = ready(i - 1)

            @pl.when(done > m_new)
            def _():
                start = lax.div(part * s, nf)

                def new_piece(r, carry):
                    act(r, m_new, across + r - start)
                    return carry

                lax.fori_loop(start, lax.div((part + 1) * s, nf), new_piece, 0)

    for n in range(chunks):
        b_local(n).start()

    def begin(s, carry):
        h_start(s)
        return carry

    lax.fori_loop(0, min(AHEAD, cases), begin, 0)
    high, low = split(table[...])
    th[...] = high
    tl_[...] = low

    def tick(step, carry):
        t = step - nf * LEAD
        i = lax.div(step, nf) - LEAD
        tau = lax.rem(step, nf)

        @pl.when(jnp.logical_and(tau == 0, jnp.logical_and(i >= 0, i < cases)))
        def _():
            if AHEAD < cases:
                @pl.when(i + AHEAD < cases)
                def _():
                    h_start(i + AHEAD)
            for d in range(1, np_):
                q = lax.rem(p + d, np_)
                h_copy(i, q, q).wait_recv()
            h_local(i).wait()
            with jax.named_scope('dft'):
              spec[lax.rem(i, RING)] = dot3((th[...], tl_[...]), split(h2[i]))

        with jax.named_scope('send'):
            send(t)

        @pl.when(jnp.logical_and(tau == nf - 2, jnp.logical_and(i >= 1, i <= cases)))
        def _():
            @pl.when(i == 1)
            def _():
                for n in range(chunks):
                    b_local(n).wait()

            with jax.named_scope('finalize'):
                finalize(i - 1)

        with jax.named_scope('pass'):
            units(t - 1, pass_on)
        with jax.named_scope('fit'):
            units(t, compute)
        return carry

    lax.fori_loop(0, nf * (LEAD + cases + 2) - 1, tick, 0)

    total = cases * pieces

    def finish(e, carry):
        acc = pland[e, chip]
        for d in range(1, chips):
            c = lax.rem(chip + d, chips)
            f_copy(e, c, c).wait_recv()
            acc = acc + fland[e, c]
        pland[e, chip] = acc
        o_copy(e).start()
        return carry

    with jax.named_scope('finish'):
        lax.fori_loop(0, total, finish, 0)

    def drain(s, carry):
        for d in range(1, np_):
            h_copy(s, lax.rem(p + d, np_), p).wait_send()
        for d in range(1, nf):
            @pl.when(me + d <= nf - 1)
            def _():
                r_copy(s, me + d, me + d, right).wait_send()

            @pl.when(me - d >= 0)
            def _():
                r_copy(s, me - d, me - d, left).wait_send()
        return carry

    lax.fori_loop(0, cases, drain, 0)
    for g in range(nf):
        @pl.when(jnp.logical_and(g <= me, has_r))
        def _():
            for n in range(chunks):
                b_copy(g, n, right, b_send_r).wait_send()

        @pl.when(jnp.logical_and(g >= me, has_l))
        def _():
            for n in range(chunks):
                b_copy(g, n, left, b_send_l).wait_send()

    def drain_out(e, carry):
        for d in range(1, chips):
            f_copy(e, lax.rem(chip + d, chips), chip).wait_send()
        o_copy(e).wait()
        return carry

    lax.fori_loop(0, total, drain_out, 0)


def local(histories, point_weight, basis):
    nf = lax.axis_size("freq")
    np_ = lax.axis_size("pts")
    cases, time_local, all_points = histories.shape
    points = all_points // np_
    plane_time = time_local * np_
    rows = 2 * F // nf
    ho = basis.shape[1] * nf // np_
    pieces = ho // COLS
    chunks = np_ // nf * pieces
    chips = np_ // 2
    total = cases * pieces
    slots = -(-pieces // nf) + -(-cases // nf)
    times = lax.axis_index("freq") * plane_time + jnp.arange(plane_time, dtype=jnp.int32)
    table = make_table(times, plane_time * nf, F, nf)
    f32, bf16 = jnp.float32, jnp.bfloat16
    hbm = pl.BlockSpec(memory_space=pl.ANY)
    vmem = pl.BlockSpec(memory_space=pltpu.VMEM)
    dma = pltpu.SemaphoreType.DMA
    coeffs = pl.pallas_call(
        functools.partial(kernel, nf, np_),
        out_shape=jax.ShapeDtypeStruct((cases * rows, ho), f32),
        in_specs=[hbm, vmem, vmem, hbm],
        out_specs=hbm,
        scratch_shapes=[
            pltpu.VMEM((cases, plane_time, points), f32),
            pltpu.VMEM((np_, pieces, points, COLS), f32),
            pltpu.VMEM((cases, nf + 1, rows, points), f32),
            pltpu.VMEM((RING, 2 * F, points), f32),
            pltpu.VMEM((rows, points), f32),
            pltpu.VMEM((2 * F, plane_time), bf16),
            pltpu.VMEM((2 * F, plane_time), bf16),
            pltpu.VMEM((cases, rows, points), bf16),
            pltpu.VMEM((cases, rows, points), bf16),
            pltpu.VMEM((slots, chips, rows, COLS), f32),
            pltpu.VMEM((slots, chips, rows, COLS), f32),
            pltpu.VMEM((total, chips, rows, COLS), f32),
            pltpu.VMEM((total, chips, rows, COLS), f32),
            dma((cases, np_)), dma((cases, np_)), dma((cases,)),
            dma((nf, chunks)), dma((nf, chunks)), dma((nf, chunks)), dma((chunks,)),
            dma((cases, nf)), dma((cases, nf + 1)),
            dma((slots,)), dma((total,)),
            dma((total, chips)), dma((total, chips)), dma((total,)),
        ],
        compiler_params=pltpu.CompilerParams(
            collective_id=0, has_side_effects=True, vmem_limit_bytes=60 * 1024 * 1024
        ),
    )(histories, table, point_weight.reshape(1, -1), basis)
    return coeffs.reshape(cases, 2, rows // 2, ho)


def solution(mesh):
    return jax.shard_map(
        local,
        mesh=mesh,
        in_specs=(P(None, ("freq", "pts"), None), P("pts"), P("pts", "freq")),
        out_specs=P(None, None, "freq", "pts"),
        check_vma=False,
    )
```

```python
import functools
import math

import jax
import jax.numpy as jnp
from jax import lax
from jax.experimental import pallas as pl
from jax.experimental.pallas import tpu as pltpu
from jax.sharding import PartitionSpec as P

F = 256
LEAD = 2
LATE = 2
RELAY = 4
AHEAD = 8
COLS = 128
RING = 2
MESH = pl.DeviceIdType.MESH


def split(x):
    high = x.astype(jnp.bfloat16)
    return high, (x - high.astype(jnp.float32)).astype(jnp.bfloat16)


def dot3(a, b):
    ah, al = a
    bh, bl = b
    dot = functools.partial(jnp.dot, preferred_element_type=jnp.float32)
    return dot(ah, bh) + (dot(ah, bl) + dot(al, bh))


def kernel(
    nf, np_, hist, weight, basis, out,
    h2, bas, rs, spec, wf, th, tl_, wh, wl, stage, pland, fland,
    h_send, h_recv, h_own, b_send_r, b_send_l, b_recv, b_own,
    r_send, r_recv, p_send, p_recv, f_send, f_recv, o_sem,
):
    cases, time_local, _ = hist.shape
    points = h2.shape[2]
    rows = wh.shape[1]
    per = np_ // nf
    pieces = bas.shape[1]
    ho = pieces * COLS
    chunks = per * pieces
    chips = np_ // 2
    me = lax.axis_index("freq")
    p = lax.axis_index("pts")
    core = lax.rem(p, 2)
    chip = lax.div(p, 2)
    right, left = jnp.minimum(me + 1, nf - 1), jnp.maximum(me - 1, 0)
    has_r, has_l = me < nf - 1, me > 0

    barrier = pltpu.get_barrier_semaphore()
    for d in range(1, np_):
        pl.semaphore_signal(barrier, inc=1, device_id={"pts": lax.rem(p + d, np_)}, device_id_type=MESH)

    @pl.when(has_r)
    def _():
        pl.semaphore_signal(barrier, inc=1, device_id={"freq": right}, device_id_type=MESH)

    @pl.when(has_l)
    def _():
        pl.semaphore_signal(barrier, inc=1, device_id={"freq": left}, device_id_type=MESH)

    inner = jnp.logical_and(has_l, has_r)

    @pl.when(inner)
    def _():
        pl.semaphore_wait(barrier, np_ + 1)

    @pl.when(jnp.logical_not(inner))
    def _():
        pl.semaphore_wait(barrier, np_)

    def h_copy(s, q, slot):
        return pltpu.make_async_remote_copy(
            src_ref=hist.at[s, :, pl.ds(pl.multiple_of(q * points, 128), points)],
            dst_ref=h2.at[s, pl.ds(pl.multiple_of(slot * time_local, 8), time_local), :],
            send_sem=h_send.at[s, q], recv_sem=h_recv.at[s, slot],
            device_id={"pts": q}, device_id_type=MESH,
        )

    def h_local(s):
        return pltpu.make_async_copy(
            hist.at[s, :, pl.ds(pl.multiple_of(p * points, 128), points)],
            h2.at[s, pl.ds(pl.multiple_of(p * time_local, 8), time_local), :],
            h_own.at[s],
        )

    def h_start(s):
        for d in range(1, np_):
            h_copy(s, lax.rem(p + d, np_), p).start()
        h_local(s).start()

    def b_source(n):
        at = lax.rem(n, per) * ho + lax.div(n, per) * COLS
        return basis.at[:, pl.ds(pl.multiple_of(at, 128), COLS)]

    def b_place(b, n):
        return bas.at[b * per + lax.rem(n, per), lax.div(n, per)]

    def b_copy(b, n, to, sems, src=None):
        dst = b_place(b, n)
        return pltpu.make_async_remote_copy(
            src_ref=dst if src is None else src, dst_ref=dst,
            send_sem=sems.at[b, n], recv_sem=b_recv.at[b, n],
            device_id={"freq": to}, device_id_type=MESH,
        )

    def b_head(n):
        @pl.when(has_r)
        def _():
            b_copy(me, n, right, b_send_r, b_source(n)).start()

        @pl.when(has_l)
        def _():
            b_copy(me, n, left, b_send_l, b_source(n)).start()

    def b_local(n):
        return pltpu.make_async_copy(b_source(n), b_place(me, n), b_own.at[n])

    def r_copy(s, g, dst, to):
        return pltpu.make_async_remote_copy(
            src_ref=rs.at[s, g], dst_ref=rs.at[s, dst], send_sem=r_send.at[s, g], recv_sem=r_recv.at[s, dst],
            device_id={"freq": to}, device_id_type=MESH,
        )

    def own(s, g):
        return spec[lax.rem(s, RING), pl.ds(pl.multiple_of(g * rows, 8), rows), :]

    def place_in(t, hops):
        u = t - 2 * hops + nf * (LEAD + 2)
        return lax.div(u, nf) - (LEAD + 2), lax.rem(u, nf)

    def forward(k, g, behind, ahead, has_ahead, to, sems, last):
        sums = jnp.logical_and(jnp.logical_and(has_ahead, ahead), jnp.logical_and(k >= 0, k < cases))

        @pl.when(sums)
        def _():
            @pl.when(behind)
            def _():
                r_copy(k, g, g, to).wait_recv()
                rs[k, g] = rs[k, g] + own(k, g)

            @pl.when(jnp.logical_not(behind))
            def _():
                rs[k, g] = own(k, g)

            if last is None:
                r_copy(k, g, g, to).start()
            else:
                @pl.when(last)
                def _():
                    r_copy(k, g, nf, to).start()

                @pl.when(jnp.logical_not(last))
                def _():
                    r_copy(k, g, g, to).start()

        n = k + LEAD
        chunk = jnp.logical_and(jnp.logical_and(jnp.logical_not(ahead), has_ahead), jnp.logical_and(n >= 0, n < chunks))

        @pl.when(jnp.logical_and(chunk, jnp.logical_and(g == me, k >= 0)))
        def _():
            b_copy(me, n, to, sems, b_source(n)).start()

        @pl.when(jnp.logical_and(chunk, g != me))
        def _():
            copy = b_copy(g, n, to, sems)
            copy.wait_recv()
            copy.start()

    def send(t):
        k, r = place_in(t, me)
        g = nf - 1 - r
        forward(k, g, has_l, g > me, has_r, right, b_send_r, None)
        k, g = place_in(t, nf - 1 - me)
        forward(k, g, has_r, g < me, has_l, left, b_send_l, g == me - 1)

    def take(n):
        @pl.when(jnp.logical_not(has_r))
        def _():
            for b in range(nf - 1):
                b_copy(b, n, right, b_send_r).wait_recv()

        @pl.when(jnp.logical_not(has_l))
        def _():
            for b in range(1, nf):
                b_copy(b, n, left, b_send_l).wait_recv()

    def finalize(s):
        at = lax.rem(s, RING + 1)

        @pl.when(has_l)
        def _():
            r_copy(s, me, me, right).wait_recv()
            wf[at] = wf[at] + rs[s, me]

        @pl.when(has_r)
        def _():
            r_copy(s, nf, nf, left).wait_recv()
            wf[at] = wf[at] + rs[s, nf]

        high, low = split(wf[at] * weight[...])
        wh[s] = high
        wl[s] = low

    def p_copy(e, slot):
        return pltpu.make_async_remote_copy(
            src_ref=stage.at[slot], dst_ref=pland.at[e],
            send_sem=p_send.at[slot], recv_sem=p_recv.at[e],
            device_id={"pts": chip * 2 + 1 - core}, device_id_type=MESH,
        )

    lines = chips // 2
    cy, cx = lax.div(chip, 2), lax.rem(chip, 2)
    beside = cy * 2 + 1 - cx

    def f_copy(e, c, to, slot):
        return pltpu.make_async_remote_copy(
            src_ref=pland.at[e, c], dst_ref=fland.at[e, slot], send_sem=f_send.at[e, c], recv_sem=f_recv.at[e, slot],
            device_id={"pts": to * 2 + core}, device_id_type=MESH,
        )

    def landed(e, slot):
        f_copy(e, beside, beside, slot).wait_recv()
        return fland[e, slot]

    def others():
        return [lax.rem(cy + d, lines) for d in range(1, lines)]

    def o_copy(e):
        s, m = lax.div(e, pieces), lax.rem(e, pieces)
        return pltpu.make_async_copy(
            pland.at[e, chip],
            out.at[pl.ds(pl.multiple_of(s * rows, 8), rows), pl.ds(pl.multiple_of(m * COLS, 128), COLS)],
            o_sem.at[e],
        )

    def compute(s, n, slot):
        m, target = lax.div(n, 2), lax.rem(n, 2)
        lhs = wh[s], wl[s]
        for c in range(0, chips, 2):
            pair = jnp.concatenate([bas[c * 2 + target, m], bas[c * 2 + 2 + target, m]], axis=1)
            both = dot3(lhs, split(pair))
            stage[slot, c] = both[:, :COLS]
            stage[slot, c + 1] = both[:, COLS:]

        @pl.when(target != core)
        def _():
            p_copy(s * pieces + m, slot).start()

    def pass_on(s, n, slot):
        m, target = lax.div(n, 2), lax.rem(n, 2)

        @pl.when(target != core)
        def _():
            p_copy(s * pieces + m, slot).wait_send()

        @pl.when(target == core)
        def _():
            spread(s, m, slot)

    def spread(s, m, slot):
        e = s * pieces + m
        p_copy(e, slot).wait_recv()
        pland[e] = pland[e] + stage[slot]
        turn = lax.rem(s + m, 2)

        @pl.when(turn == 0)
        def _():
            for row in others() + [cy]:
                f_copy(e, row * 2 + 1 - cx, beside, row).start()

        @pl.when(turn == 1)
        def _():
            for row in others():
                f_copy(e, row * 2 + 1 - cx, row * 2 + cx, cy * 2 + 1).start()
                f_copy(e, row * 2 + cx, row * 2 + cx, cy * 2).start()

    def relay(s, n, slot):
        @pl.when(lax.rem(n, 2) == core)
        def _():
            turn_over(s, lax.div(n, 2))

    def turn_over(s, m):
        e = s * pieces + m
        turn = lax.rem(s + m, 2)

        @pl.when(turn == 0)
        def _():
            for row in others():
                c = row * 2 + cx
                pland[e, c] = pland[e, c] + landed(e, row)
                f_copy(e, c, c, lines + cy).start()

        @pl.when(turn == 1)
        def _():
            for row in others():
                pland[e, beside] = pland[e, beside] + landed(e, row * 2 + 1)
            f_copy(e, beside, beside, cy * 2).start()

    def ready(i):
        return jnp.minimum(i + LEAD - 1, chunks)

    def new_chunk(i, act):
        def cases_of(n, carry):
            def one(s, inner_carry):
                act(s, n, s)
                return inner_carry

            return lax.fori_loop(0, i - 1, one, carry)

        lax.fori_loop(ready(i - 1), ready(i), cases_of, 0)

    def new_case(i, act):
        def one(n, carry):
            act(i - 1, n, cases - 1 + n)
            return carry

        lax.fori_loop(0, ready(i), one, 0)

    between = jnp.minimum(me, 1) * jnp.minimum(nf - 1 - me, 1)

    def slot_of(t):
        v = t - (nf - 2 + LATE) + 3 * between + nf * (LEAD + 3)
        return lax.div(v, nf) - (LEAD + 3), lax.rem(v, nf)

    for n in range(min(LEAD, chunks)):
        b_head(n)

    def begin(s, carry):
        h_start(s)
        return carry

    lax.fori_loop(0, min(AHEAD, cases), begin, 0)
    for n in range(chunks):
        b_local(n).start()

    plane_time = h2.shape[1]
    total_time = plane_time * nf
    half = rows // 2
    unit = 2.0 * math.pi / total_time
    times = me * plane_time + lax.broadcasted_iota(jnp.int32, (half, plane_time), 1)
    bins = lax.broadcasted_iota(jnp.int32, (half, plane_time), 0) + 1
    scale = (0.5 - 0.5 * jnp.cos(unit * times[:8].astype(jnp.float32)))[:1] / math.sqrt(total_time)

    def tabulate(g, carry):
        angle = unit * lax.rem(times * (bins + g * half), total_time).astype(jnp.float32)
        for c, wave in enumerate((jnp.cos(angle) * scale, -jnp.sin(angle) * scale)):
            at = pl.ds(pl.multiple_of(g * rows + c * half, 16), half)
            high, low = split(wave)
            th[at, :] = high
            tl_[at, :] = low
        return carry

    with jax.named_scope('table'):
        lax.fori_loop(0, nf, tabulate, 0)

    def drain_inputs():
        def drain(s, carry):
            for d in range(1, np_):
                h_copy(s, lax.rem(p + d, np_), p).wait_send()
            for d in range(1, nf):
                @pl.when(me + d <= nf - 1)
                def _():
                    r_copy(s, me + d, me + d, right).wait_send()

                @pl.when(me - d >= 0)
                def _():
                    r_copy(s, me - d, me - d, left).wait_send()
            return carry

        lax.fori_loop(0, cases, drain, 0)
        for g in range(nf):
            @pl.when(jnp.logical_and(g <= me, has_r))
            def _():
                for n in range(chunks):
                    b_copy(g, n, right, b_send_r).wait_send()

            @pl.when(jnp.logical_and(g >= me, has_l))
            def _():
                for n in range(chunks):
                    b_copy(g, n, left, b_send_l).wait_send()

    def tick(step, carry):
        t = step - nf * LEAD
        i = lax.div(step, nf) - LEAD
        tau = lax.rem(step, nf)

        @pl.when(jnp.logical_and(tau == 0, jnp.logical_and(i >= 0, i < cases)))
        def _():
            if AHEAD < cases:
                @pl.when(i + AHEAD < cases)
                def _():
                    h_start(i + AHEAD)
            for d in range(1, np_):
                q = lax.rem(p + d, np_)
                h_copy(i, q, q).wait_recv()
            h_local(i).wait()
            with jax.named_scope('dft'):
              spec[lax.rem(i, RING)] = dot3((th[...], tl_[...]), split(h2[i]))
            wf[lax.rem(i, RING + 1)] = own(i, me)

        with jax.named_scope('send'):
            send(t)

        j, part = slot_of(t)
        live = jnp.logical_and(j >= 1, j <= cases)

        @pl.when(jnp.logical_and(part == 0, live))
        def _():
            @pl.when(j == 1)
            def _():
                for n in range(chunks):
                    b_local(n).wait()

            @pl.when(jnp.logical_or(jnp.logical_not(has_r), jnp.logical_not(has_l)))
            def _():
                def taken(n, carry):
                    take(n)
                    return carry

                lax.fori_loop(ready(j - 1) * jnp.minimum(j - 1, 1), ready(j), taken, 0)

            with jax.named_scope('fitB'):
                new_chunk(j, compute)
            with jax.named_scope('finalize'):
                finalize(j - 1)
        @pl.when(jnp.logical_and(part == 1, live))
        def _():
            with jax.named_scope('passB'):
                new_chunk(j, pass_on)
            with jax.named_scope('fitA'):
                new_case(j, compute)

        @pl.when(jnp.logical_and(part == 2, live))
        def _():
            with jax.named_scope('passA'):
                new_case(j, pass_on)

        @pl.when(jnp.logical_and(part == 2, j == cases + 1))
        def _():
            with jax.named_scope('drain'):
                drain_inputs()

        def relays(i, carry):
            new_chunk(i, relay)
            new_case(i, relay)
            return carry

        @pl.when(jnp.logical_and(part == 3, jnp.logical_and(j >= RELAY, j <= cases + 1)))
        def _():
            with jax.named_scope('relay'):
                lax.fori_loop((j - 1) * jnp.minimum(j - RELAY, 1) + (1 - jnp.minimum(j - RELAY, 1)), j, relays, 0)

        return carry

    lax.fori_loop(0, nf * (LEAD + cases + 2) + LATE + 2, tick, 0)

    total = cases * pieces

    def finish(e, carry):
        turn = lax.rem(lax.div(e, pieces) + lax.rem(e, pieces), 2)

        with jax.named_scope('fwait'):
            @pl.when(turn == 0)
            def _():
                acc = pland[e, chip] + landed(e, cy)
                for row in others():
                    acc = acc + landed(e, lines + row)
                pland[e, chip] = acc

            @pl.when(turn == 1)
            def _():
                acc = pland[e, chip]
                for row in others() + [cy]:
                    acc = acc + landed(e, row * 2)
                pland[e, chip] = acc

        o_copy(e).start()
        return carry

    with jax.named_scope('finish'):
        lax.fori_loop(0, total, finish, 0)

    def drain_out(e, carry):
        for d in range(1, chips):
            c = lax.rem(chip + d, chips)
            f_copy(e, c, c, chip).wait_send()
        o_copy(e).wait()
        return carry

    lax.fori_loop(0, total, drain_out, 0)


def local(histories, point_weight, basis):
    nf = lax.axis_size("freq")
    np_ = lax.axis_size("pts")
    cases, time_local, all_points = histories.shape
    points = all_points // np_
    plane_time = time_local * np_
    rows = 2 * F // nf
    ho = basis.shape[1] * nf // np_
    pieces = ho // COLS
    chunks = np_ // nf * pieces
    chips = np_ // 2
    total = cases * pieces
    slots = cases - 1 + chunks
    assert np_ == 2 * nf
    f32, bf16 = jnp.float32, jnp.bfloat16
    hbm = pl.BlockSpec(memory_space=pl.ANY)
    vmem = pl.BlockSpec(memory_space=pltpu.VMEM)
    dma = pltpu.SemaphoreType.DMA
    coeffs = pl.pallas_call(
        functools.partial(kernel, nf, np_),
        out_shape=jax.ShapeDtypeStruct((cases * rows, ho), f32),
        in_specs=[hbm, vmem, hbm],
        out_specs=hbm,
        scratch_shapes=[
            pltpu.VMEM((cases, plane_time, points), f32),
            pltpu.VMEM((np_, pieces, points, COLS), f32),
            pltpu.VMEM((cases, nf + 1, rows, points), f32),
            pltpu.VMEM((RING, 2 * F, points), f32),
            pltpu.VMEM((RING + 1, rows, points), f32),
            pltpu.VMEM((2 * F, plane_time), bf16),
            pltpu.VMEM((2 * F, plane_time), bf16),
            pltpu.VMEM((cases, rows, points), bf16),
            pltpu.VMEM((cases, rows, points), bf16),
            pltpu.VMEM((slots, chips, rows, COLS), f32),
            pltpu.VMEM((total, chips, rows, COLS), f32),
            pltpu.VMEM((total, chips, rows, COLS), f32),
            dma((cases, np_)), dma((cases, np_)), dma((cases,)),
            dma((nf, chunks)), dma((nf, chunks)), dma((nf, chunks)), dma((chunks,)),
            dma((cases, nf)), dma((cases, nf + 1)),
            dma((slots,)), dma((total,)),
            dma((total, chips)), dma((total, chips)), dma((total,)),
        ],
        compiler_params=pltpu.CompilerParams(
            collective_id=0, has_side_effects=True, vmem_limit_bytes=65000 * 1024
        ),
    )(histories, point_weight.reshape(1, -1), basis)
    return coeffs.reshape(cases, 2, rows // 2, ho)


def solution(mesh):
    return jax.shard_map(
        local,
        mesh=mesh,
        in_specs=(P(None, ("freq", "pts"), None), P("pts"), P("pts", "freq")),
        out_specs=P(None, None, "freq", "pts"),
        check_vma=False,
    )
```

```python
import functools
import math

import jax
import jax.numpy as jnp
from jax import lax
from jax.experimental import pallas as pl
from jax.experimental.pallas import tpu as pltpu
from jax.sharding import PartitionSpec as P

F = 256
LEAD = 2
LATE = 2
RELAY = 4
AHEAD = 8
BEHIND = 3
COLS = 128
RING = 2
MESH = pl.DeviceIdType.MESH


def split(x):
    high = x.astype(jnp.bfloat16)
    return high, (x - high.astype(jnp.float32)).astype(jnp.bfloat16)


def dot3(a, b):
    ah, al = a
    bh, bl = b
    dot = functools.partial(jnp.dot, preferred_element_type=jnp.float32)
    return dot(ah, bh) + (dot(ah, bl) + dot(al, bh))


def kernel(
    nf, np_, hist, weight, basis, out,
    h2, bas, rs, spec, wf, th, tl_, wt, stage, pland, fland,
    h_send, h_recv, b_send_r, b_send_l, b_recv, b_own,
    r_send, r_recv, p_send, p_recv, f_send, f_recv, o_sem,
):
    cases, time_local, _ = hist.shape
    points = h2.shape[2]
    rows = rs.shape[2]
    per = np_ // nf
    pieces = bas.shape[1]
    ho = pieces * COLS
    chunks = per * pieces
    chips = np_ // 2
    me = lax.axis_index("freq")
    p = lax.axis_index("pts")
    core = lax.rem(p, 2)
    chip = lax.div(p, 2)
    right, left = jnp.minimum(me + 1, nf - 1), jnp.maximum(me - 1, 0)
    has_r, has_l = me < nf - 1, me > 0

    barrier = pltpu.get_barrier_semaphore()
    for d in range(1, np_):
        pl.semaphore_signal(barrier, inc=1, device_id={"pts": lax.rem(p + d, np_)}, device_id_type=MESH)

    @pl.when(has_r)
    def _():
        pl.semaphore_signal(barrier, inc=1, device_id={"freq": right}, device_id_type=MESH)

    @pl.when(has_l)
    def _():
        pl.semaphore_signal(barrier, inc=1, device_id={"freq": left}, device_id_type=MESH)

    inner = jnp.logical_and(has_l, has_r)

    @pl.when(inner)
    def _():
        pl.semaphore_wait(barrier, np_ + 1)

    @pl.when(jnp.logical_not(inner))
    def _():
        pl.semaphore_wait(barrier, np_)

    def h_copy(s, q, slot):
        return pltpu.make_async_remote_copy(
            src_ref=hist.at[s, :, pl.ds(pl.multiple_of(q * points, 128), points)],
            dst_ref=h2.at[s, pl.ds(pl.multiple_of(slot * time_local, 8), time_local), :],
            send_sem=h_send, recv_sem=h_recv.at[s],
            device_id={"pts": q}, device_id_type=MESH,
        )

    def h_local(s):
        return pltpu.make_async_copy(
            hist.at[s, :, pl.ds(pl.multiple_of(p * points, 128), points)],
            h2.at[s, pl.ds(pl.multiple_of(p * time_local, 8), time_local), :],
            h_recv.at[s],
        )

    def whole_copy(ref, sem):
        return pltpu.make_async_copy(ref, ref, sem)

    def h_start(s):
        for d in range(1, np_):
            h_copy(s, lax.rem(p + d, np_), p).start()
        h_local(s).start()

    def b_source(n):
        at = lax.rem(n, per) * ho + lax.div(n, per) * COLS
        return basis.at[:, pl.ds(pl.multiple_of(at, 128), COLS)]

    def b_place(b, n):
        return bas.at[b * per + lax.rem(n, per), lax.div(n, per)]

    def b_copy(b, n, to, sems, src=None):
        dst = b_place(b, n)
        return pltpu.make_async_remote_copy(
            src_ref=dst if src is None else src, dst_ref=dst,
            send_sem=sems.at[b], recv_sem=b_recv.at[b, n],
            device_id={"freq": to}, device_id_type=MESH,
        )

    def b_head(n):
        @pl.when(has_r)
        def _():
            b_copy(me, n, right, b_send_r, b_source(n)).start()

        @pl.when(has_l)
        def _():
            b_copy(me, n, left, b_send_l, b_source(n)).start()

    def b_local(n):
        return pltpu.make_async_copy(b_source(n), b_place(me, n), b_own)

    def r_copy(s, g, dst, to):
        return pltpu.make_async_remote_copy(
            src_ref=rs.at[s, g], dst_ref=rs.at[s, dst], send_sem=r_send, recv_sem=r_recv.at[s, dst],
            device_id={"freq": to}, device_id_type=MESH,
        )

    def own(s, g):
        return spec[lax.rem(s, RING), pl.ds(pl.multiple_of(g * rows, 8), rows), :]

    def place_in(t, hops):
        u = t - 2 * hops + nf * (LEAD + 2)
        return lax.div(u, nf) - (LEAD + 2), lax.rem(u, nf)

    def forward(k, g, behind, ahead, has_ahead, to, sems, last):
        sums = jnp.logical_and(jnp.logical_and(has_ahead, ahead), jnp.logical_and(k >= 0, k < cases))

        @pl.when(sums)
        def _():
            @pl.when(behind)
            def _():
                r_copy(k, g, g, to).wait_recv()
                rs[k, g] = rs[k, g] + own(k, g)

            @pl.when(jnp.logical_not(behind))
            def _():
                rs[k, g] = own(k, g)

            if last is None:
                r_copy(k, g, g, to).start()
            else:
                @pl.when(last)
                def _():
                    r_copy(k, g, nf, to).start()

                @pl.when(jnp.logical_not(last))
                def _():
                    r_copy(k, g, g, to).start()

        n = k + LEAD
        chunk = jnp.logical_and(jnp.logical_and(jnp.logical_not(ahead), has_ahead), jnp.logical_and(n >= 0, n < chunks))

        @pl.when(jnp.logical_and(chunk, jnp.logical_and(g == me, k >= 0)))
        def _():
            b_copy(me, n, to, sems, b_source(n)).start()

        @pl.when(jnp.logical_and(chunk, g != me))
        def _():
            copy = b_copy(g, n, to, sems)
            copy.wait_recv()
            copy.start()

    def send(t):
        k, r = place_in(t, me)
        g = nf - 1 - r
        forward(k, g, has_l, g > me, has_r, right, b_send_r, None)
        k, g = place_in(t, nf - 1 - me)
        forward(k, g, has_r, g < me, has_l, left, b_send_l, g == me - 1)

    def take(n):
        @pl.when(jnp.logical_not(has_r))
        def _():
            for b in range(nf - 1):
                b_copy(b, n, right, b_send_r).wait_recv()

        @pl.when(jnp.logical_not(has_l))
        def _():
            for b in range(1, nf):
                b_copy(b, n, left, b_send_l).wait_recv()

    def finalize(s):
        at = lax.rem(s, RING + 1)

        @pl.when(has_l)
        def _():
            r_copy(s, me, me, right).wait_recv()
            wf[at] = wf[at] + rs[s, me]

        @pl.when(has_r)
        def _():
            r_copy(s, nf, nf, left).wait_recv()
            wf[at] = wf[at] + rs[s, nf]

        high, low = split(wf[at] * weight[...])
        wt[s, :rows] = high
        wt[s, rows:] = low

    def p_copy(e, slot):
        return pltpu.make_async_remote_copy(
            src_ref=stage.at[slot], dst_ref=pland.at[e],
            send_sem=p_send.at[slot], recv_sem=p_recv.at[e],
            device_id={"pts": chip * 2 + 1 - core}, device_id_type=MESH,
        )

    lines = chips // 2
    cy, cx = lax.div(chip, 2), lax.rem(chip, 2)
    beside = cy * 2 + 1 - cx

    def f_copy(e, c, to, slot, leg):
        return pltpu.make_async_remote_copy(
            src_ref=pland.at[e, c], dst_ref=fland.at[e, slot], send_sem=f_send, recv_sem=f_recv.at[e, leg],
            device_id={"pts": to * 2 + core}, device_id_type=MESH,
        )

    def landed(e, leg):
        whole_copy(fland.at[e, pl.ds(0, lines - 1 + leg)], f_recv.at[e, leg]).wait()

    def others():
        return [lax.rem(cy + d, lines) for d in range(1, lines)]

    def o_copy(e):
        s, m = lax.div(e, pieces), lax.rem(e, pieces)
        return pltpu.make_async_copy(
            pland.at[e, chip],
            out.at[pl.ds(pl.multiple_of(s * rows, 8), rows), pl.ds(pl.multiple_of(m * COLS, 128), COLS)],
            o_sem,
        )

    def compute(s, n, slot):
        m, target = lax.div(n, 2), lax.rem(n, 2)
        lhs = wt[s]
        dot = functools.partial(jnp.dot, preferred_element_type=jnp.float32)
        for c in range(0, chips, 2):
            pair = jnp.concatenate([bas[c * 2 + target, m], bas[c * 2 + 2 + target, m]], axis=1)
            high, low = split(pair)
            tall = dot(lhs, high)
            both = tall[:rows] + (dot(lhs[:rows], low) + tall[rows:])
            stage[slot, c] = both[:, :COLS]
            stage[slot, c + 1] = both[:, COLS:]

        @pl.when(target != core)
        def _():
            p_copy(s * pieces + m, slot).start()

    def pass_on(s, n, slot):
        m, target = lax.div(n, 2), lax.rem(n, 2)

        @pl.when(target != core)
        def _():
            p_copy(s * pieces + m, slot).wait_send()

        @pl.when(target == core)
        def _():
            spread(s, m, slot)

    def spread(s, m, slot):
        e = s * pieces + m
        p_copy(e, slot).wait_recv()
        pland[e] = pland[e] + stage[slot]
        turn = lax.rem(s + m, 2)

        @pl.when(turn == 0)
        def _():
            for row in others():
                f_copy(e, row * 2 + 1 - cx, beside, row, 0).start()
            f_copy(e, beside, beside, cy, 1).start()

        @pl.when(turn == 1)
        def _():
            for row in others():
                f_copy(e, row * 2 + 1 - cx, row * 2 + cx, cy * 2 + 1, 0).start()
                f_copy(e, row * 2 + cx, row * 2 + cx, cy * 2, 1).start()

    def relay(s, n, slot):
        @pl.when(lax.rem(n, 2) == core)
        def _():
            turn_over(s, lax.div(n, 2))

    def turn_over(s, m):
        e = s * pieces + m
        turn = lax.rem(s + m, 2)
        landed(e, 0)

        @pl.when(turn == 0)
        def _():
            for row in others():
                c = row * 2 + cx
                pland[e, c] = pland[e, c] + fland[e, row]
                f_copy(e, c, c, lines + cy, 1).start()

        @pl.when(turn == 1)
        def _():
            for row in others():
                pland[e, beside] = pland[e, beside] + fland[e, row * 2 + 1]
            f_copy(e, beside, beside, cy * 2, 1).start()

    def ready(i):
        return jnp.minimum(i + LEAD - 1, chunks)

    def new_chunk(i, act):
        def cases_of(n, carry):
            def one(s, inner_carry):
                act(s, n, s)
                return inner_carry

            return lax.fori_loop(0, i - 1, one, carry)

        lax.fori_loop(ready(i - 1), ready(i), cases_of, 0)

    def new_case(i, act, low=0):
        def one(n, carry):
            act(i - 1, n, cases - 1 + n)
            return carry

        lax.fori_loop(low, ready(i), one, 0)

    between = jnp.minimum(me, 1) * jnp.minimum(nf - 1 - me, 1)

    def slot_of(t):
        v = t - (nf - 2 + LATE) + 3 * between + nf * (LEAD + 3)
        return lax.div(v, nf) - (LEAD + 3), lax.rem(v, nf)

    for n in range(min(LEAD, chunks)):
        b_head(n)

    def begin(s, carry):
        h_start(s)
        return carry

    lax.fori_loop(0, min(AHEAD, cases), begin, 0)
    for n in range(chunks):
        b_local(n).start()

    plane_time = h2.shape[1]
    total_time = plane_time * nf
    half = rows // 2
    unit = 2.0 * math.pi / total_time
    times = me * plane_time + lax.broadcasted_iota(jnp.int32, (half, plane_time), 1)
    bins = lax.broadcasted_iota(jnp.int32, (half, plane_time), 0) + 1
    scale = (0.5 - 0.5 * jnp.cos(unit * times[:8].astype(jnp.float32)))[:1] / math.sqrt(total_time)

    def tabulate(g, carry):
        angle = unit * lax.rem(times * (bins + g * half), total_time).astype(jnp.float32)
        for c, wave in enumerate((jnp.cos(angle) * scale, -jnp.sin(angle) * scale)):
            at = pl.ds(pl.multiple_of(g * rows + c * half, 16), half)
            high, low = split(wave)
            th[at, :] = high
            tl_[at, :] = low
        return carry

    with jax.named_scope('table'):
        lax.fori_loop(0, nf, tabulate, 0)

    def drain_inputs():
        whole_copy(h2.at[:, pl.ds(0, time_local * (np_ - 1))], h_send).wait()
        whole_copy(rs.at[:, pl.ds(0, nf - 1)], r_send).wait()
        for g in range(nf):
            block = bas.at[pl.ds(g * per, per)]

            @pl.when(jnp.logical_and(g <= me, has_r))
            def _():
                whole_copy(block, b_send_r.at[g]).wait()

            @pl.when(jnp.logical_and(g >= me, has_l))
            def _():
                whole_copy(block, b_send_l.at[g]).wait()

    def tick(step, carry):
        t = step - nf * LEAD
        i = lax.div(step, nf) - LEAD
        tau = lax.rem(step, nf)

        @pl.when(jnp.logical_and(tau == 0, jnp.logical_and(i >= 0, i < cases)))
        def _():
            if AHEAD < cases:
                @pl.when(i + AHEAD < cases)
                def _():
                    h_start(i + AHEAD)
            whole_copy(h2.at[i], h_recv.at[i]).wait()
            with jax.named_scope('dft'):
              spec[lax.rem(i, RING)] = dot3((th[...], tl_[...]), split(h2[i]))
            wf[lax.rem(i, RING + 1)] = own(i, me)

        with jax.named_scope('send'):
            send(t)

        j, part = slot_of(t)
        live = jnp.logical_and(j >= 1, j <= cases)

        @pl.when(jnp.logical_and(part == 0, live))
        def _():
            @pl.when(j == 1)
            def _():
                whole_copy(bas.at[pl.ds(me * per, per)], b_own).wait()

            @pl.when(jnp.logical_or(jnp.logical_not(has_r), jnp.logical_not(has_l)))
            def _():
                def taken(n, carry):
                    take(n)
                    return carry

                lax.fori_loop(ready(j - 1) * jnp.minimum(j - 1, 1), ready(j), taken, 0)

            with jax.named_scope('fitB'):
                new_chunk(j, compute)
            with jax.named_scope('finalize'):
                finalize(j - 1)
        @pl.when(jnp.logical_and(part == 1, live))
        def _():
            with jax.named_scope('passB'):
                new_chunk(j, pass_on)
            with jax.named_scope('fitA'):
                def fit(s, n, slot):
                    compute(s, n, slot)

                    @pl.when(n >= BEHIND)
                    def _():
                        pass_on(s, n - BEHIND, slot - BEHIND)

                new_case(j, fit)

        @pl.when(jnp.logical_and(part == 2, live))
        def _():
            with jax.named_scope('passA'):
                new_case(j, pass_on, jnp.maximum(ready(j) - BEHIND, 0))

        @pl.when(jnp.logical_and(part == 2, j == cases + 1))
        def _():
            with jax.named_scope('drain'):
                drain_inputs()

        def relays(i, carry):
            new_chunk(i, relay)
            new_case(i, relay)
            return carry

        @pl.when(jnp.logical_and(part == 3, jnp.logical_and(j >= RELAY, j <= cases + 1)))
        def _():
            with jax.named_scope('relay'):
                lax.fori_loop((j - 1) * jnp.minimum(j - RELAY, 1) + (1 - jnp.minimum(j - RELAY, 1)), j, relays, 0)

        return carry

    lax.fori_loop(0, nf * (LEAD + cases + 2) + LATE + 2, tick, 0)

    total = cases * pieces

    def finish(e, carry):
        turn = lax.rem(lax.div(e, pieces) + lax.rem(e, pieces), 2)

        landed(e, 1)

        @pl.when(turn == 0)
        def _():
            acc = pland[e, chip] + fland[e, cy]
            for row in others():
                acc = acc + fland[e, lines + row]
            pland[e, chip] = acc

        @pl.when(turn == 1)
        def _():
            acc = pland[e, chip]
            for row in others() + [cy]:
                acc = acc + fland[e, row * 2]
            pland[e, chip] = acc

        o_copy(e).start()
        return carry

    with jax.named_scope('finish'):
        lax.fori_loop(0, total, finish, 0)

    with jax.named_scope('drain_out'):
        whole_copy(pland.at[:, pl.ds(0, chips - 1)], f_send).wait()
        whole_copy(pland.at[:, 0], o_sem).wait()


def local(histories, point_weight, basis):
    nf = lax.axis_size("freq")
    np_ = lax.axis_size("pts")
    cases, time_local, all_points = histories.shape
    points = all_points // np_
    plane_time = time_local * np_
    rows = 2 * F // nf
    ho = basis.shape[1] * nf // np_
    pieces = ho // COLS
    chunks = np_ // nf * pieces
    chips = np_ // 2
    total = cases * pieces
    slots = cases - 1 + chunks
    assert np_ == 2 * nf
    f32, bf16 = jnp.float32, jnp.bfloat16
    hbm = pl.BlockSpec(memory_space=pl.ANY)
    vmem = pl.BlockSpec(memory_space=pltpu.VMEM)
    dma = pltpu.SemaphoreType.DMA
    coeffs = pl.pallas_call(
        functools.partial(kernel, nf, np_),
        out_shape=jax.ShapeDtypeStruct((cases * rows, ho), f32),
        in_specs=[hbm, vmem, hbm],
        out_specs=hbm,
        scratch_shapes=[
            pltpu.VMEM((cases, plane_time, points), f32),
            pltpu.VMEM((np_, pieces, points, COLS), f32),
            pltpu.VMEM((cases, nf + 1, rows, points), f32),
            pltpu.VMEM((RING, 2 * F, points), f32),
            pltpu.VMEM((RING + 1, rows, points), f32),
            pltpu.VMEM((2 * F, plane_time), bf16),
            pltpu.VMEM((2 * F, plane_time), bf16),
            pltpu.VMEM((cases, 2 * rows, points), bf16),
            pltpu.VMEM((slots, chips, rows, COLS), f32),
            pltpu.VMEM((total, chips, rows, COLS), f32),
            pltpu.VMEM((total, chips, rows, COLS), f32),
            dma, dma((cases,)),
            dma((nf,)), dma((nf,)), dma((nf, chunks)), dma,
            dma, dma((cases, nf + 1)),
            dma((slots,)), dma((total,)),
            dma, dma((total, 2)), dma,
        ],
        compiler_params=pltpu.CompilerParams(
            collective_id=0, has_side_effects=True, vmem_limit_bytes=65000 * 1024
        ),
    )(histories, point_weight.reshape(1, -1), basis)
    return coeffs.reshape(cases, 2, rows // 2, ho)


def solution(mesh):
    return jax.shard_map(
        local,
        mesh=mesh,
        in_specs=(P(None, ("freq", "pts"), None), P("pts"), P("pts", "freq")),
        out_specs=P(None, None, "freq", "pts"),
        check_vma=False,
    )
```

```python
import functools
import math

import jax
import jax.numpy as jnp
from jax import lax
from jax.experimental import pallas as pl
from jax.experimental.pallas import tpu as pltpu
from jax.sharding import PartitionSpec as P

F = 256
LEAD = 2
LATE = 2
RELAY = 4
AHEAD = 8
BEHIND = 3
COLS = 128
RING = 2
MESH = pl.DeviceIdType.MESH


def split(x):
    high = x.astype(jnp.bfloat16)
    return high, (x - high.astype(jnp.float32)).astype(jnp.bfloat16)


def dot3(a, b):
    ah, al = a
    bh, bl = b
    dot = functools.partial(jnp.dot, preferred_element_type=jnp.float32)
    return dot(ah, bh) + (dot(ah, bl) + dot(al, bh))


def kernel(
    nf, np_, hist, weight, basis, out,
    h2, bas, rs, spec, wf, th, tl_, wt, stage, pland, fland,
    h_send, h_recv, b_send_r, b_send_l, b_recv, b_own,
    r_send, r_recv, p_send, p_recv, f_send, f_recv, o_sem,
):
    cases, time_local, _ = hist.shape
    points = h2.shape[2]
    rows = rs.shape[2]
    per = np_ // nf
    pieces = bas.shape[1]
    ho = pieces * COLS
    chunks = per * pieces
    chips = np_ // 2
    me = lax.axis_index("freq")
    p = lax.axis_index("pts")
    core = lax.rem(p, 2)
    chip = lax.div(p, 2)
    right, left = jnp.minimum(me + 1, nf - 1), jnp.maximum(me - 1, 0)
    has_r, has_l = me < nf - 1, me > 0

    barrier = pltpu.get_barrier_semaphore()
    for d in range(1, np_):
        pl.semaphore_signal(barrier, inc=1, device_id={"pts": lax.rem(p + d, np_)}, device_id_type=MESH)

    @pl.when(has_r)
    def _():
        pl.semaphore_signal(barrier, inc=1, device_id={"freq": right}, device_id_type=MESH)

    @pl.when(has_l)
    def _():
        pl.semaphore_signal(barrier, inc=1, device_id={"freq": left}, device_id_type=MESH)

    inner = jnp.logical_and(has_l, has_r)

    @pl.when(inner)
    def _():
        pl.semaphore_wait(barrier, np_ + 1)

    @pl.when(jnp.logical_not(inner))
    def _():
        pl.semaphore_wait(barrier, np_)

    def h_copy(s, q, slot):
        return pltpu.make_async_remote_copy(
            src_ref=hist.at[s, :, pl.ds(pl.multiple_of(q * points, 128), points)],
            dst_ref=h2.at[s, pl.ds(pl.multiple_of(slot * time_local, 8), time_local), :],
            send_sem=h_send, recv_sem=h_recv.at[s],
            device_id={"pts": q}, device_id_type=MESH,
        )

    def h_local(s):
        return pltpu.make_async_copy(
            hist.at[s, :, pl.ds(pl.multiple_of(p * points, 128), points)],
            h2.at[s, pl.ds(pl.multiple_of(p * time_local, 8), time_local), :],
            h_recv.at[s],
        )

    def whole_copy(ref, sem):
        return pltpu.make_async_copy(ref, ref, sem)

    def h_start(s):
        for d in range(1, np_):
            h_copy(s, lax.rem(p + d, np_), p).start()
        h_local(s).start()

    def b_source(n):
        at = lax.rem(n, per) * ho + lax.div(n, per) * COLS
        return basis.at[:, pl.ds(pl.multiple_of(at, 128), COLS)]

    def b_place(b, n):
        return bas.at[b * per + lax.rem(n, per), lax.div(n, per)]

    def b_copy(b, n, to, sems, src=None):
        dst = b_place(b, n)
        return pltpu.make_async_remote_copy(
            src_ref=dst if src is None else src, dst_ref=dst,
            send_sem=sems.at[b], recv_sem=b_recv.at[b, n],
            device_id={"freq": to}, device_id_type=MESH,
        )

    def b_head(n):
        @pl.when(has_r)
        def _():
            b_copy(me, n, right, b_send_r, b_source(n)).start()

        @pl.when(has_l)
        def _():
            b_copy(me, n, left, b_send_l, b_source(n)).start()

    def b_local(n):
        return pltpu.make_async_copy(b_source(n), b_place(me, n), b_own)

    def r_copy(s, g, dst, to):
        return pltpu.make_async_remote_copy(
            src_ref=rs.at[s, g], dst_ref=rs.at[s, dst], send_sem=r_send, recv_sem=r_recv.at[s, dst],
            device_id={"freq": to}, device_id_type=MESH,
        )

    def own(s, g):
        return spec[lax.rem(s, RING), pl.ds(pl.multiple_of(g * rows, 8), rows), :]

    def place_in(t, hops):
        u = t - 2 * hops + nf * (LEAD + 2)
        return lax.div(u, nf) - (LEAD + 2), lax.rem(u, nf)

    def forward(k, g, behind, ahead, has_ahead, to, sems, last):
        sums = jnp.logical_and(jnp.logical_and(has_ahead, ahead), jnp.logical_and(k >= 0, k < cases))

        @pl.when(sums)
        def _():
            @pl.when(behind)
            def _():
                r_copy(k, g, g, to).wait_recv()
                rs[k, g] = rs[k, g] + own(k, g)

            @pl.when(jnp.logical_not(behind))
            def _():
                rs[k, g] = own(k, g)

            if last is None:
                r_copy(k, g, g, to).start()
            else:
                @pl.when(last)
                def _():
                    r_copy(k, g, nf, to).start()

                @pl.when(jnp.logical_not(last))
                def _():
                    r_copy(k, g, g, to).start()

        n = k + LEAD
        chunk = jnp.logical_and(jnp.logical_and(jnp.logical_not(ahead), has_ahead), jnp.logical_and(n >= 0, n < chunks))

        @pl.when(jnp.logical_and(chunk, jnp.logical_and(g == me, k >= 0)))
        def _():
            b_copy(me, n, to, sems, b_source(n)).start()

        @pl.when(jnp.logical_and(chunk, g != me))
        def _():
            copy = b_copy(g, n, to, sems)
            copy.wait_recv()
            copy.start()

    def send(t):
        k, r = place_in(t, me)
        g = nf - 1 - r
        forward(k, g, has_l, g > me, has_r, right, b_send_r, None)
        k, g = place_in(t, nf - 1 - me)
        forward(k, g, has_r, g < me, has_l, left, b_send_l, g == me - 1)

    def take(n):
        @pl.when(jnp.logical_not(has_r))
        def _():
            for b in range(nf - 1):
                b_copy(b, n, right, b_send_r).wait_recv()

        @pl.when(jnp.logical_not(has_l))
        def _():
            for b in range(1, nf):
                b_copy(b, n, left, b_send_l).wait_recv()

    def finalize(s):
        at = lax.rem(s, RING + 1)

        @pl.when(has_l)
        def _():
            r_copy(s, me, me, right).wait_recv()
            wf[at] = wf[at] + rs[s, me]

        @pl.when(has_r)
        def _():
            r_copy(s, nf, nf, left).wait_recv()
            wf[at] = wf[at] + rs[s, nf]

        high, low = split(wf[at] * weight[...])
        wt[s, :rows] = high
        wt[s, rows:] = low

    def p_copy(e, slot):
        return pltpu.make_async_remote_copy(
            src_ref=stage.at[slot], dst_ref=pland.at[e],
            send_sem=p_send.at[slot], recv_sem=p_recv.at[e],
            device_id={"pts": chip * 2 + 1 - core}, device_id_type=MESH,
        )

    lines = chips // 2
    cy, cx = lax.div(chip, 2), lax.rem(chip, 2)
    beside = cy * 2 + 1 - cx

    def f_copy(e, c, to, slot, leg):
        return pltpu.make_async_remote_copy(
            src_ref=pland.at[e, c], dst_ref=fland.at[e, slot], send_sem=f_send, recv_sem=f_recv.at[e, leg],
            device_id={"pts": to * 2 + core}, device_id_type=MESH,
        )

    def landed(e, leg):
        whole_copy(fland.at[e, pl.ds(0, lines - 1 + leg)], f_recv.at[e, leg]).wait()

    def others():
        return [lax.rem(cy + d, lines) for d in range(1, lines)]

    def o_copy(e):
        s, m = lax.div(e, pieces), lax.rem(e, pieces)
        return pltpu.make_async_copy(
            pland.at[e, chip],
            out.at[pl.ds(pl.multiple_of(s * rows, 8), rows), pl.ds(pl.multiple_of(m * COLS, 128), COLS)],
            o_sem,
        )

    def compute(s, n, slot):
        m, target = lax.div(n, 2), lax.rem(n, 2)
        lhs = wt[s]
        dot = functools.partial(jnp.dot, preferred_element_type=jnp.float32)
        for c in range(0, chips, 2):
            pair = jnp.concatenate([bas[c * 2 + target, m], bas[c * 2 + 2 + target, m]], axis=1)
            high, low = split(pair)
            tall = dot(lhs, high)
            both = tall[:rows] + (dot(lhs[:rows], low) + tall[rows:])
            stage[slot, c] = both[:, :COLS]
            stage[slot, c + 1] = both[:, COLS:]

        @pl.when(target != core)
        def _():
            p_copy(s * pieces + m, slot).start()

    def pass_on(s, n, slot):
        m, target = lax.div(n, 2), lax.rem(n, 2)

        @pl.when(target != core)
        def _():
            p_copy(s * pieces + m, slot).wait_send()

        @pl.when(target == core)
        def _():
            spread(s, m, slot)

    def spread(s, m, slot):
        e = s * pieces + m
        p_copy(e, slot).wait_recv()
        pland[e] = pland[e] + stage[slot]
        turn = lax.rem(s + m, 2)

        @pl.when(turn == 0)
        def _():
            for row in others():
                f_copy(e, row * 2 + 1 - cx, beside, row, 0).start()
            f_copy(e, beside, beside, cy, 1).start()

        @pl.when(turn == 1)
        def _():
            for row in others():
                f_copy(e, row * 2 + 1 - cx, row * 2 + cx, cy * 2 + 1, 0).start()
                f_copy(e, row * 2 + cx, row * 2 + cx, cy * 2, 1).start()

    def relay(s, n, slot):
        @pl.when(lax.rem(n, 2) == core)
        def _():
            turn_over(s, lax.div(n, 2))

    def turn_over(s, m):
        e = s * pieces + m
        turn = lax.rem(s + m, 2)
        landed(e, 0)

        @pl.when(turn == 0)
        def _():
            for row in others():
                c = row * 2 + cx
                pland[e, c] = pland[e, c] + fland[e, row]
                f_copy(e, c, c, lines + cy, 1).start()

        @pl.when(turn == 1)
        def _():
            for row in others():
                pland[e, beside] = pland[e, beside] + fland[e, row * 2 + 1]
            f_copy(e, beside, beside, cy * 2, 1).start()

    def ready(i):
        return jnp.minimum(i + LEAD - 1, chunks)

    def new_chunk(i, act):
        def cases_of(n, carry):
            def one(s, inner_carry):
                act(s, n, s)
                return inner_carry

            return lax.fori_loop(0, i - 1, one, carry)

        lax.fori_loop(ready(i - 1), ready(i), cases_of, 0)

    def new_case(i, act, low=0):
        def one(n, carry):
            act(i - 1, n, cases - 1 + n)
            return carry

        lax.fori_loop(low, ready(i), one, 0)

    between = jnp.minimum(me, 1) * jnp.minimum(nf - 1 - me, 1)

    def slot_of(t):
        v = t - (nf - 2 + LATE) + 3 * between + nf * (LEAD + 3)
        return lax.div(v, nf) - (LEAD + 3), lax.rem(v, nf)

    for n in range(min(LEAD, chunks)):
        b_head(n)

    def begin(s, carry):
        h_start(s)
        return carry

    lax.fori_loop(0, min(AHEAD, cases), begin, 0)
    for n in range(chunks):
        b_local(n).start()

    plane_time = h2.shape[1]
    total_time = plane_time * nf
    half = rows // 2
    unit = 2.0 * math.pi / total_time
    times = me * plane_time + lax.broadcasted_iota(jnp.int32, (half, plane_time), 1)
    bins = lax.broadcasted_iota(jnp.int32, (half, plane_time), 0) + 1
    scale = (0.5 - 0.5 * jnp.cos(unit * times[:8].astype(jnp.float32)))[:1] / math.sqrt(total_time)

    def tabulate(g, carry):
        angle = unit * lax.rem(times * (bins + g * half), total_time).astype(jnp.float32)
        for c, wave in enumerate((jnp.cos(angle) * scale, -jnp.sin(angle) * scale)):
            at = pl.ds(pl.multiple_of(g * rows + c * half, 16), half)
            high, low = split(wave)
            th[at, :] = high
            tl_[at, :] = low
        return carry

    with jax.named_scope('table'):
        lax.fori_loop(0, nf, tabulate, 0)

    def drain_inputs():
        whole_copy(h2.at[:, pl.ds(0, time_local * (np_ - 1))], h_send).wait()
        whole_copy(rs.at[:, pl.ds(0, nf - 1)], r_send).wait()
        for g in range(nf):
            block = bas.at[pl.ds(g * per, per)]

            @pl.when(jnp.logical_and(g <= me, has_r))
            def _():
                whole_copy(block, b_send_r.at[g]).wait()

            @pl.when(jnp.logical_and(g >= me, has_l))
            def _():
                whole_copy(block, b_send_l.at[g]).wait()

    def tick(step, carry):
        t = step - nf * LEAD
        i = lax.div(step, nf) - LEAD
        tau = lax.rem(step, nf)

        @pl.when(jnp.logical_and(tau == 0, jnp.logical_and(i >= 0, i < cases)))
        def _():
            if AHEAD < cases:
                @pl.when(i + AHEAD < cases)
                def _():
                    h_start(i + AHEAD)
            whole_copy(h2.at[i], h_recv.at[i]).wait()
            with jax.named_scope('dft'):
              spec[lax.rem(i, RING)] = dot3((th[...], tl_[...]), split(h2[i]))
            wf[lax.rem(i, RING + 1)] = own(i, me)

        with jax.named_scope('send'):
            send(t)

        j, part = slot_of(t)
        live = jnp.logical_and(j >= 1, j <= cases)

        def relays(i, carry):
            new_chunk(i, relay)
            new_case(i, relay)
            return carry

        @pl.when(jnp.logical_and(part == 0, j == cases))
        def _():
            with jax.named_scope('relayB'):
                lax.fori_loop(cases - 1, cases, relays, 0)

        @pl.when(jnp.logical_and(part == 0, live))
        def _():
            @pl.when(j == 1)
            def _():
                whole_copy(bas.at[pl.ds(me * per, per)], b_own).wait()

            @pl.when(jnp.logical_or(jnp.logical_not(has_r), jnp.logical_not(has_l)))
            def _():
                def taken(n, carry):
                    take(n)
                    return carry

                lax.fori_loop(ready(j - 1) * jnp.minimum(j - 1, 1), ready(j), taken, 0)

            with jax.named_scope('fitB'):
                new_chunk(j, compute)
            with jax.named_scope('finalize'):
                finalize(j - 1)
        @pl.when(jnp.logical_and(part == 1, live))
        def _():
            with jax.named_scope('passB'):
                new_chunk(j, pass_on)
            with jax.named_scope('fitA'):
                def fit(s, n, slot):
                    compute(s, n, slot)

                    @pl.when(n >= BEHIND)
                    def _():
                        pass_on(s, n - BEHIND, slot - BEHIND)

                new_case(j, fit)

        @pl.when(jnp.logical_and(part == 2, live))
        def _():
            with jax.named_scope('passA'):
                new_case(j, pass_on, jnp.maximum(ready(j) - BEHIND, 0))

        @pl.when(jnp.logical_and(part == 2, j == cases + 1))
        def _():
            with jax.named_scope('drain'):
                drain_inputs()

        @pl.when(jnp.logical_and(jnp.logical_and(part == 3, j != cases), jnp.logical_and(j >= RELAY, j <= cases + 1)))
        def _():
            with jax.named_scope('relay'):
                lax.fori_loop((j - 1) * jnp.minimum(j - RELAY, 1) + (1 - jnp.minimum(j - RELAY, 1)), j, relays, 0)

        return carry

    lax.fori_loop(0, nf * (LEAD + cases + 2) + LATE + 2, tick, 0)

    total = cases * pieces

    def finish(e, carry):
        turn = lax.rem(lax.div(e, pieces) + lax.rem(e, pieces), 2)

        landed(e, 1)

        @pl.when(turn == 0)
        def _():
            acc = pland[e, chip] + fland[e, cy]
            for row in others():
                acc = acc + fland[e, lines + row]
            pland[e, chip] = acc

        @pl.when(turn == 1)
        def _():
            acc = pland[e, chip]
            for row in others() + [cy]:
                acc = acc + fland[e, row * 2]
            pland[e, chip] = acc

        o_copy(e).start()
        return carry

    with jax.named_scope('finish'):
        lax.fori_loop(0, total, finish, 0)

    with jax.named_scope('drain_out'):
        whole_copy(pland.at[:, pl.ds(0, chips - 1)], f_send).wait()
        whole_copy(pland.at[:, 0], o_sem).wait()


def local(histories, point_weight, basis):
    nf = lax.axis_size("freq")
    np_ = lax.axis_size("pts")
    cases, time_local, all_points = histories.shape
    points = all_points // np_
    plane_time = time_local * np_
    rows = 2 * F // nf
    ho = basis.shape[1] * nf // np_
    pieces = ho // COLS
    chunks = np_ // nf * pieces
    chips = np_ // 2
    total = cases * pieces
    slots = cases - 1 + chunks
    assert np_ == 2 * nf
    f32, bf16 = jnp.float32, jnp.bfloat16
    hbm = pl.BlockSpec(memory_space=pl.ANY)
    vmem = pl.BlockSpec(memory_space=pltpu.VMEM)
    dma = pltpu.SemaphoreType.DMA
    coeffs = pl.pallas_call(
        functools.partial(kernel, nf, np_),
        out_shape=jax.ShapeDtypeStruct((cases * rows, ho), f32),
        in_specs=[hbm, vmem, hbm],
        out_specs=hbm,
        scratch_shapes=[
            pltpu.VMEM((cases, plane_time, points), f32),
            pltpu.VMEM((np_, pieces, points, COLS), f32),
            pltpu.VMEM((cases, nf + 1, rows, points), f32),
            pltpu.VMEM((RING, 2 * F, points), f32),
            pltpu.VMEM((RING + 1, rows, points), f32),
            pltpu.VMEM((2 * F, plane_time), bf16),
            pltpu.VMEM((2 * F, plane_time), bf16),
            pltpu.VMEM((cases, 2 * rows, points), bf16),
            pltpu.VMEM((slots, chips, rows, COLS), f32),
            pltpu.VMEM((total, chips, rows, COLS), f32),
            pltpu.VMEM((total, chips, rows, COLS), f32),
            dma, dma((cases,)),
            dma((nf,)), dma((nf,)), dma((nf, chunks)), dma,
            dma, dma((cases, nf + 1)),
            dma((slots,)), dma((total,)),
            dma, dma((total, 2)), dma,
        ],
        compiler_params=pltpu.CompilerParams(
            collective_id=0, has_side_effects=True, vmem_limit_bytes=65000 * 1024
        ),
    )(histories, point_weight.reshape(1, -1), basis)
    return coeffs.reshape(cases, 2, rows // 2, ho)


def solution(mesh):
    return jax.shard_map(
        local,
        mesh=mesh,
        in_specs=(P(None, ("freq", "pts"), None), P("pts"), P("pts", "freq")),
        out_specs=P(None, None, "freq", "pts"),
        check_vma=False,
    )
```
